128 devices in a mesh: samp: 8 (over z, core), pix: 16 (over x, y).
Axes of the slice: x: 4, y: 4, z: 4, core: 2. Of those that a mesh axis runs over, the one named last changes fastest.
Arguments:
- stamps: bfloat16 [8192, 16384], P(('samp', 'pix')), may hold values from -6 to 6
- start_panel: float32 [16384, 32], P('pix'), may hold values from -0.046875 to 0.046875
Outputs:
- eigen_psfs: float32 [16384, 32], P('pix')
The draws below stay inside these ranges and needn't reach their ends.
All inputs are finite; a program needn't handle non-finite values.
Results may differ from the reference program's by a relative error of at most 0.025.
Values may be sent and summed in bfloat16 or wider, within the bound.
A program may use at most 64 MiB of HBM per device.

```python
import math
import jax
import jax.numpy as jnp
from jax import lax

PIX = 16384
K = 32
ITERS = 10
SAMPLES = 8192


def draw_stamps(key, part):
    first = jax.random.fold_in(jax.random.fold_in(key, 7), 0)
    values = jax.random.normal(first, (SAMPLES, PIX), jnp.float32)
    return jnp.clip(values, -6.0, 6.0).astype(jnp.bfloat16)


def block_levels(rng, shape, cuts, least, top_value):
    def one(axis_at, parts):
        draws = jax.random.uniform(jax.random.fold_in(jax.random.fold_in(rng, 6), axis_at), (parts,), jnp.float32, least / len(cuts), top_value / len(cuts))
        return jnp.repeat(jnp.exp(draws), shape[axis_at] // parts).reshape((-1,) + (1,) * (len(shape) - axis_at - 1))

    loudness = one(*cuts[0])
    for cut in cuts[1:]:
        loudness = loudness * one(*cut)
    return loudness


def bell_draw(key, shape, deviation, most, shards=(), dtype=jnp.bfloat16):
    drawn = deviation * jax.random.normal(key, shape, jnp.float32)
    if shards:
        drawn = drawn * block_levels(key, shape, shards, -0.22, 0.18)
    return jnp.clip(drawn, -most, most).astype(dtype)


def setup_inputs(seed: int = 0) -> dict:
    arg_keys = jax.random.split(jax.random.key(seed), 3)
    return {
        "stamps": draw_stamps(jax.random.fold_in(arg_keys[2], 71), 0),
        "start_panel": bell_draw(arg_keys[1], (PIX, K), PIX ** -0.5, 0.046875, ((0, 16),), jnp.float32),
    }


def reference(stamps, start_panel):
    panel = start_panel
    for step in range(ITERS):
        proj = jnp.dot(stamps.astype(jnp.float32), panel.astype(jnp.bfloat16).astype(jnp.float32), preferred_element_type=jnp.float32).astype(jnp.bfloat16)
        back = lax.dot_general(stamps.astype(jnp.float32), proj.astype(jnp.float32), (((0,), (0,)), ((), ())), preferred_element_type=jnp.float32)
        gram = jnp.dot(back.T, back, precision=lax.Precision.HIGHEST)
        lower = jnp.linalg.cholesky(gram)
        panel = lax.linalg.triangular_solve(lower, back, left_side=False, lower=True, transpose_a=True)
    return panel * math.sqrt(PIX)
```

```python
import functools

import jax
import jax.numpy as jnp
from jax import lax
from jax.experimental import pallas as pl
from jax.experimental.pallas import tpu as pltpu
from jax.sharding import PartitionSpec as P

PIX = 16384
K = 32
ITERS = 10
SCALE = 128.0
GX, GY = 4, 4
NP = GX * GY
NS = 8
ROWS = 64
SB = NP * ROWS
PB = PIX // NP
HK = K // 2
MESH = pl.DeviceIdType.MESH
NT = (((1,), (1,)), ((), ()))
BF, F32 = jnp.bfloat16, jnp.float32

PIX_STEPS = sorted(
    ((dx, dy) for dx in range(GX) for dy in range(GY) if dx or dy),
    key=lambda d: -(min(d[0], GX - d[0]) + min(d[1], GY - d[1])),
)
SAMP_STEPS = [4, 5, 3, 2, 6, 7, 1]


def split3(a):
    hi = a.astype(BF)
    rest = a - hi.astype(F32)
    mid = rest.astype(BF)
    return hi, mid, (rest - mid.astype(F32)).astype(BF)


def inverse_cholesky(gram):
    rows = lax.broadcasted_iota(jnp.int32, (K, K), 0)
    cols = lax.broadcasted_iota(jnp.int32, (K, K), 1)
    work = jnp.concatenate([gram, jnp.where(rows == cols, 1.0, 0.0).astype(F32)], axis=1)
    below = lax.broadcasted_iota(jnp.int32, (K, 1), 0)
    for j in range(K):
        pivot = lax.rsqrt(work[j : j + 1, j : j + 1])
        row = work[j : j + 1, :] * pivot
        column = work[:, j : j + 1] * pivot
        work = jnp.where(
            below > j, work - column * row, jnp.where(below == j, row, work)
        )
    return work[:, K:]


def pack_gram(gram):
    return jnp.concatenate([gram[8 * i : 8 * i + 8, :] for i in range(4)], axis=1)


def unpack_gram(packed):
    return jnp.concatenate([packed[:, K * i : K * i + K] for i in range(4)], axis=0)


def kernel(
    stamps, start, out,
    block, blockt, panel, part1, got1, proj, gram_out, gram_in, part2, got2,
    sems, gram_sems,
):
    s, p = lax.axis_index("samp"), lax.axis_index("pix")
    x, y = p // GY, p % GY

    def pix_peer(dx, dy):
        return ((x + dx) % GX) * GY + (y + dy) % GY

    def samp_peer(d):
        return (s + d) % NS

    def send(src, dst, sem, arrived=None, **device):
        pltpu.make_async_remote_copy(
            src_ref=src, dst_ref=dst, send_sem=sems.at[sem],
            recv_sem=sems.at[sem + 1] if arrived is None else arrived,
            device_id=device, device_id_type=MESH,
        ).start()

    def wait_on(ref, sem):
        pltpu.make_async_copy(ref, ref, sem).wait()

    def wait(ref, sem):
        wait_on(ref, sems.at[sem])

    barrier = pltpu.get_barrier_semaphore()
    for dx, dy in PIX_STEPS:
        pl.semaphore_signal(barrier, inc=1, device_id={"pix": pix_peer(dx, dy)}, device_id_type=MESH)
    for d in SAMP_STEPS:
        pl.semaphore_signal(barrier, inc=1, device_id={"samp": samp_peer(d)}, device_id_type=MESH)
    pl.semaphore_wait(barrier, NP - 1 + NS - 1)

    mine = block.at[pl.ds(pl.multiple_of(p * ROWS, ROWS), ROWS)]

    def pixels_of(q):
        return stamps.at[:, pl.ds(pl.multiple_of(q * PB, PB), PB)]

    for dx, dy in PIX_STEPS:
        q = pix_peer(dx, dy)
        send(pixels_of(q), mine, 0, pix=q)
    own = pltpu.make_async_copy(pixels_of(p), mine, sems.at[14])
    own.start()

    first = start[...].T.astype(BF)
    for i in range(NS):
        panel[i] = first[:, 128 * i : 128 * i + 128]

    own.wait()
    wait(block.at[pl.ds(0, SB - ROWS)], 1)
    wait(block.at[pl.ds(0, SB - ROWS)], 0)
    blockt[...] = block[...].T

    def whole_panel():
        return jnp.concatenate([panel[i] for i in range(NS)], axis=1)

    def share_gram(slot, partial):
        gram_out[...] = pack_gram(partial)
        for i, (dx, dy) in enumerate(PIX_STEPS):
            send(gram_out, gram_in.at[slot, i], 4, gram_sems.at[slot], pix=pix_peer(dx, dy))

    def sum_gram(slot):
        wait_on(gram_in.at[slot], gram_sems.at[slot])
        total = gram_out[...]
        for i in range(NP - 1):
            total = total + gram_in[slot, i]
        wait(gram_in.at[slot], 4)
        return unpack_gram(total)

    def gram_of(now):
        return lax.dot_general(now, now, NT, preferred_element_type=F32)

    def sweep(step, carry):
        now = whole_panel()
        partial = jnp.dot(now, blockt[...], preferred_element_type=F32).astype(BF)
        for q in range(NP):
            c, h = q // 2, q % 2
            part1[q] = partial[HK * h : HK * h + HK, 128 * c : 128 * c + 128]
        for i, (dx, dy) in enumerate(PIX_STEPS):
            q = pix_peer(dx, dy)
            send(part1.at[q], got1.at[i], 2, pix=q)
        rows = lax.broadcasted_iota(jnp.int32, (K, K), 0)
        cols = lax.broadcasted_iota(jnp.int32, (K, K), 1)
        unit = jnp.where(rows == cols, 1.0 / NP, 0.0).astype(F32)
        slot = lax.rem(step, 2)
        share_gram(slot, jnp.where(step == 0, unit, gram_of(now)))

        wait(got1, 3)
        total = part1[p].astype(F32)
        for i in range(NP - 1):
            total = total + got1[i].astype(F32)
        proj[p] = total.astype(BF)
        for dx, dy in PIX_STEPS:
            send(proj.at[p], proj.at[p], 6, pix=pix_peer(dx, dy))
        wait(got1, 2)

        hi, mid, low = split3(inverse_cholesky(sum_gram(slot)))
        left = jnp.concatenate([hi, mid, low], axis=1)

        wait(proj.at[pl.ds(0, NP - 1)], 7)
        wait(proj.at[pl.ds(0, NP - 1)], 6)
        raw = jnp.concatenate(
            [jnp.concatenate([proj[2 * c], proj[2 * c + 1]], axis=0) for c in range(NP // 2)], axis=1
        )
        scaled = jnp.dot(
            left, jnp.concatenate([raw, raw, raw], axis=0), preferred_element_type=F32
        ).astype(BF)
        back = jnp.dot(scaled, block[...], preferred_element_type=F32).astype(BF)
        for r in range(NS):
            part2[r] = back[:, 128 * r : 128 * r + 128]
        for i, d in enumerate(SAMP_STEPS):
            r = samp_peer(d)
            send(part2.at[r], got2.at[i], 8, samp=r)
        wait(got2, 9)
        total = part2[s].astype(F32)
        for i in range(NS - 1):
            total = total + got2[i].astype(F32)
        panel[s] = total.astype(BF)
        for d in SAMP_STEPS:
            send(panel.at[s], panel.at[s], 10, samp=samp_peer(d))
        wait(got2, 8)
        wait(panel.at[pl.ds(0, NS - 1)], 11)
        wait(panel.at[pl.ds(0, NS - 1)], 10)
        return carry

    lax.fori_loop(0, ITERS, sweep, 0)

    now = whole_panel()
    share_gram(ITERS % 2, gram_of(now))
    hi, mid, low = split3(inverse_cholesky(sum_gram(ITERS % 2)) * SCALE)
    left = jnp.concatenate([hi, mid, low], axis=1)
    out[...] = jnp.dot(left, jnp.concatenate([now, now, now], axis=0), preferred_element_type=F32)


def local(stamps, start_panel):
    vmem = pl.BlockSpec(memory_space=pltpu.VMEM)
    result = pl.pallas_call(
        kernel,
        out_shape=jax.ShapeDtypeStruct((K, PB), F32),
        in_specs=[pl.BlockSpec(memory_space=pl.ANY), vmem],
        out_specs=vmem,
        scratch_shapes=[
            pltpu.VMEM((SB, PB), BF),
            pltpu.VMEM((PB, SB), BF),
            pltpu.VMEM((NS, K, 128), BF),
            pltpu.VMEM((NP, HK, 128), BF),
            pltpu.VMEM((NP - 1, HK, 128), BF),
            pltpu.VMEM((NP, HK, 128), BF),
            pltpu.VMEM((8, 128), F32),
            pltpu.VMEM((2, NP - 1, 8, 128), F32),
            pltpu.VMEM((NS, K, 128), BF),
            pltpu.VMEM((NS - 1, K, 128), BF),
            pltpu.SemaphoreType.DMA((15,)),
            pltpu.SemaphoreType.DMA((2,)),
        ],
        compiler_params=pltpu.CompilerParams(
            collective_id=0, has_side_effects=True, vmem_limit_bytes=48 << 20
        ),
    )(stamps, start_panel)
    return result.T


def solution(mesh):
    return jax.shard_map(
        local,
        mesh=mesh,
        in_specs=(P(("samp", "pix"), None), P("pix", None)),
        out_specs=P("pix", None),
        check_vma=False,
    )
```

```python
import jax
import jax.numpy as jnp
from jax import lax
from jax.experimental import pallas as pl
from jax.experimental.pallas import tpu as pltpu
from jax.sharding import PartitionSpec as P

PIX = 16384
K = 32
ITERS = 10
SCALE = 128.0
GX, GY, GZ = 4, 4, 4
CHIPS = GX * GY
ROWS = 64
SB = CHIPS * 2 * ROWS
PC = PIX // CHIPS
PB = PC // 2
HK = K // 2
LANES = 128
TILES = PB // LANES
MESH = pl.DeviceIdType.MESH
NT = (((1,), (1,)), ((), ()))
BF, F32 = jnp.bfloat16, jnp.float32


def hops(offset):
    return sum(min(d, 4 - d) for d in offset)


OFFSETS = sorted(((dx, dy) for dx in range(GX) for dy in range(GY)), key=hops)
BACK = [OFFSETS.index(((-dx) % GX, (-dy) % GY)) for dx, dy in OFFSETS]
FAR_FIRST = list(range(CHIPS - 1, 0, -1))
Z_STEPS = [2, 1, 3]


def split3(a):
    hi = a.astype(BF)
    rest = a - hi.astype(F32)
    mid = rest.astype(BF)
    return hi, mid, (rest - mid.astype(F32)).astype(BF)


def inverse_cholesky(gram):
    rows = lax.broadcasted_iota(jnp.int32, (K, K), 0)
    cols = lax.broadcasted_iota(jnp.int32, (K, K), 1)
    work = jnp.concatenate([gram, jnp.where(rows == cols, 1.0, 0.0).astype(F32)], axis=1)
    below = lax.broadcasted_iota(jnp.int32, (K, 1), 0)
    for j in range(K):
        pivot = lax.rsqrt(work[j : j + 1, j : j + 1])
        row = work[j : j + 1, :] * pivot
        column = work[:, j : j + 1] * pivot
        work = jnp.where(
            below > j, work - column * row, jnp.where(below == j, row, work)
        )
    return work[:, K:]


def apply_factor(factor, value):
    f, v = split3(factor), split3(value)
    pairs = [(0, 0), (0, 1), (1, 0), (1, 1), (0, 2), (2, 0)]
    left = jnp.concatenate([f[i] for i, _ in pairs], axis=1)
    right = jnp.concatenate([v[j] for _, j in pairs], axis=0)
    return jnp.dot(left, right, preferred_element_type=F32)


def pack_gram(gram):
    return jnp.concatenate([gram[8 * i : 8 * i + 8, :] for i in range(4)], axis=1)


def unpack_gram(packed):
    return jnp.concatenate([packed[:, K * i : K * i + K] for i in range(4)], axis=0)


def kernel(
    stamps, start, out,
    block, blockt, panel, part1, got1, proj, gram_out, gram_core, gram_chip, gram_in, sums, pair,
    sems, core_sems, gram_sems, z_sems,
):
    s, p = lax.axis_index("samp"), lax.axis_index("pix")
    x, y, z, c = p // GY, p % GY, s // 2, s % 2

    def device(slot, core):
        dx, dy = OFFSETS[slot]
        return {"samp": z * 2 + core, "pix": ((x + dx) % GX) * GY + (y + dy) % GY}

    def at_z(dz):
        return {"samp": ((z + dz) % GZ) * 2 + c, "pix": p}

    other = 1 - c

    def send(src, dst, sem, to, arrived=None):
        pltpu.make_async_remote_copy(
            src_ref=src, dst_ref=dst, send_sem=sems.at[sem],
            recv_sem=sems.at[sem + 1] if arrived is None else arrived,
            device_id=to, device_id_type=MESH,
        ).start()

    def wait_on(ref, sem):
        pltpu.make_async_copy(ref, ref, sem).wait()

    def wait(ref, sem):
        wait_on(ref, sems.at[sem])

    barrier = pltpu.get_barrier_semaphore()
    for slot in FAR_FIRST:
        for core in range(2):
            pl.semaphore_signal(barrier, inc=1, device_id=device(slot, core), device_id_type=MESH)
    for dz in Z_STEPS:
        pl.semaphore_signal(barrier, inc=1, device_id=at_z(dz), device_id_type=MESH)
    pl.semaphore_signal(barrier, inc=1, device_id=device(0, other), device_id_type=MESH)
    pl.semaphore_wait(barrier, 2 * CHIPS - 1 + GZ - 1)

    def rows_of(slot):
        return block.at[pl.ds(pl.multiple_of(slot * 2 * ROWS + c * ROWS, ROWS), ROWS)]

    def pixels_of(to, core):
        return stamps.at[:, pl.ds(pl.multiple_of(to["pix"] * PC + core * PB, PB), PB)]

    for slot in FAR_FIRST:
        for core in range(2):
            to = device(slot, core)
            send(pixels_of(to, core), rows_of(BACK[slot]), 0, to)
    to = device(0, other)
    send(pixels_of(to, other), rows_of(0), 0, to)
    own = pltpu.make_async_copy(pixels_of(device(0, c), c), rows_of(0), sems.at[14])
    own.start()

    panel[...] = start[:, pl.ds(pl.multiple_of(c * PB, PB), PB)].astype(BF)

    own.wait()
    wait(block.at[pl.ds(0, SB - ROWS)], 1)
    wait(block.at[pl.ds(0, SB - ROWS)], 0)
    blockt[...] = block[...].T

    def share_gram(turn, partial):
        gram_out[...] = pack_gram(partial)
        send(gram_out, gram_core.at[turn], 4, device(0, other), core_sems.at[turn])

    def share_chip_gram(turn):
        wait_on(gram_core.at[turn], core_sems.at[turn])
        gram_chip[...] = gram_out[...] + gram_core[turn]
        wait(gram_out, 4)
        for slot in FAR_FIRST:
            send(gram_chip, gram_in.at[turn, BACK[slot] - 1], 6, device(slot, c), gram_sems.at[turn])

    def sum_gram(turn):
        wait_on(gram_in.at[turn], gram_sems.at[turn])
        total = gram_chip[...]
        for i in range(CHIPS - 1):
            total = total + gram_in[turn, i]
        wait(gram_in.at[turn], 6)
        return unpack_gram(total)

    def gram_of(now):
        return lax.dot_general(now, now, NT, preferred_element_type=F32)

    def sweep(step, carry):
        turn = lax.rem(step, 2)
        now = panel[...]
        for group in (1, 0):
            first = group * CHIPS // 2
            lanes = pl.ds(first * LANES, CHIPS // 2 * LANES)
            partial = jnp.dot(now, blockt[:, lanes], preferred_element_type=F32).astype(BF)
            for i in range(CHIPS // 2):
                for core in range(2):
                    part1[first + i, core] = partial[HK * core : HK * core + HK, LANES * i : LANES * i + LANES]
            for slot in range(first + CHIPS // 2 - 1, first - 1, -1):
                if slot:
                    for core in range(2):
                        send(part1.at[slot, core], got1.at[BACK[slot] * 2 - 1 + c], 2, device(slot, core))
        send(part1.at[0, other], got1.at[0], 2, device(0, other))
        rows = lax.broadcasted_iota(jnp.int32, (K, K), 0)
        cols = lax.broadcasted_iota(jnp.int32, (K, K), 1)
        unit = jnp.where(rows == cols, 1.0 / (2 * CHIPS), 0.0).astype(F32)
        share_gram(turn, jnp.where(step == 0, unit, gram_of(now)))

        wait(got1, 3)
        total = part1[0, c].astype(F32)
        for i in range(2 * CHIPS - 1):
            total = total + got1[i].astype(F32)
        proj[0, c] = total.astype(BF)
        for slot in FAR_FIRST:
            for core in range(2):
                send(proj.at[0, c], proj.at[BACK[slot], c], 8, device(slot, core))
        send(proj.at[0, c], proj.at[0, c], 8, device(0, other))
        wait(got1, 2)
        share_chip_gram(turn)

        wait(got1, 9)
        wait(got1, 8)
        raw = jnp.concatenate(
            [jnp.concatenate([proj[i, 0], proj[i, 1]], axis=0) for i in range(CHIPS)], axis=1
        )
        back = jnp.dot(raw, block[...], preferred_element_type=F32).astype(BF)
        sums[turn, z] = back
        for dz in Z_STEPS:
            send(sums.at[turn, z], sums.at[turn, z], 10, at_z(dz), z_sems.at[turn])

        factor = inverse_cholesky(sum_gram(turn))
        wait_on(sums.at[turn, pl.ds(0, GZ - 1)], z_sems.at[turn])
        wait(sums.at[turn, pl.ds(0, GZ - 1)], 10)
        total = sums[turn, 0].astype(F32)
        for i in range(1, GZ):
            total = total + sums[turn, i].astype(F32)
        panel[...] = apply_factor(factor, total).astype(BF)
        return carry

    lax.fori_loop(0, ITERS, sweep, 0)

    now = panel[...]
    send(panel, pair, 12, device(0, other))
    share_gram(ITERS % 2, gram_of(now))
    share_chip_gram(ITERS % 2)
    wait(pair, 13)
    wait(pair, 12)
    factor = inverse_cholesky(sum_gram(ITERS % 2)) * SCALE
    out[:, pl.ds(pl.multiple_of(c * PB, PB), PB)] = apply_factor(factor, now.astype(F32))
    out[:, pl.ds(pl.multiple_of(other * PB, PB), PB)] = apply_factor(factor, pair[...].astype(F32))


def local(stamps, start_panel):
    vmem = pl.BlockSpec(memory_space=pltpu.VMEM)
    result = pl.pallas_call(
        kernel,
        out_shape=jax.ShapeDtypeStruct((K, PC), F32),
        in_specs=[pl.BlockSpec(memory_space=pltpu.HBM), vmem],
        out_specs=vmem,
        scratch_shapes=[
            pltpu.VMEM((SB, PB), BF),
            pltpu.VMEM((PB, SB), BF),
            pltpu.VMEM((K, PB), BF),
            pltpu.VMEM((CHIPS, 2, HK, LANES), BF),
            pltpu.VMEM((2 * CHIPS - 1, HK, LANES), BF),
            pltpu.VMEM((CHIPS, 2, HK, LANES), BF),
            pltpu.VMEM((8, LANES), F32),
            pltpu.VMEM((2, 8, LANES), F32),
            pltpu.VMEM((8, LANES), F32),
            pltpu.VMEM((2, CHIPS - 1, 8, LANES), F32),
            pltpu.VMEM((2, GZ, K, PB), BF),
            pltpu.VMEM((K, PB), BF),
            pltpu.SemaphoreType.DMA((15,)),
            pltpu.SemaphoreType.DMA((2,)),
            pltpu.SemaphoreType.DMA((2,)),
            pltpu.SemaphoreType.DMA((2,)),
        ],
        compiler_params=pltpu.CompilerParams(
            collective_id=0, has_side_effects=True, vmem_limit_bytes=63 << 20
        ),
    )(stamps, start_panel.T)
    return result.T


def solution(mesh):
    return jax.shard_map(
        local,
        mesh=mesh,
        in_specs=(P(("samp", "pix"), None), P("pix", None)),
        out_specs=P("pix", None),
        check_vma=False,
    )
```

```python
import jax
import jax.numpy as jnp
from jax import lax
from jax.experimental import pallas as pl
from jax.experimental.pallas import tpu as pltpu
from jax.sharding import PartitionSpec as P

PIX = 16384
K = 32
ITERS = 10
SCALE = 128.0
GX, GY, GZ = 4, 4, 4
CHIPS = GX * GY
ROWS = 64
SB = CHIPS * 2 * ROWS
PC = PIX // CHIPS
PB = PC // 2
HK = K // 2
LANES = 128
TILES = PB // LANES
MESH = pl.DeviceIdType.MESH
NT = (((1,), (1,)), ((), ()))
BF, F32 = jnp.bfloat16, jnp.float32


def hops(offset):
    return sum(min(d, 4 - d) for d in offset)


OFFSETS = sorted(((dx, dy) for dx in range(GX) for dy in range(GY)), key=hops)
BACK = [OFFSETS.index(((-dx) % GX, (-dy) % GY)) for dx, dy in OFFSETS]
FAR_FIRST = list(range(CHIPS - 1, 0, -1))
GROUPS = [(0, 4), (4, 10), (10, 14), (14, 16)]
GROUP_OF = [g for g, (first, last) in enumerate(GROUPS) for _ in range(first, last)]
Z_STEPS = [2, 1, 3]


def split3(a):
    hi = a.astype(BF)
    rest = a - hi.astype(F32)
    mid = rest.astype(BF)
    return hi, mid, (rest - mid.astype(F32)).astype(BF)


def inverse_cholesky(gram):
    rows = lax.broadcasted_iota(jnp.int32, (K, K), 0)
    cols = lax.broadcasted_iota(jnp.int32, (K, K), 1)
    work = jnp.concatenate([gram, jnp.where(rows == cols, 1.0, 0.0).astype(F32)], axis=1)
    below = lax.broadcasted_iota(jnp.int32, (K, 1), 0)
    for j in range(0, K, 2):
        one, two = work[j : j + 1, :], work[j + 1 : j + 2, :]
        pivot = lax.rsqrt(one[:, j : j + 1])
        under = two[:, j : j + 1] * pivot
        pivot2 = lax.rsqrt(two[:, j + 1 : j + 2] - under * under)
        row = one * pivot
        row2 = (two - under * row) * pivot2
        column = work[:, j : j + 1] * pivot
        column2 = (work[:, j + 1 : j + 2] - under * column) * pivot2
        rest = work - column * row - column2 * row2
        work = jnp.where(
            below > j + 1, rest, jnp.where(below == j, row, jnp.where(below == j + 1, row2, work))
        )
    return work[:, K:]


def apply_factor(factor, value):
    f, v = split3(factor), split3(value)
    pairs = [(0, 0), (0, 1), (1, 0), (1, 1), (0, 2), (2, 0)]
    left = jnp.concatenate([f[i] for i, _ in pairs], axis=1)
    right = jnp.concatenate([v[j] for _, j in pairs], axis=0)
    return jnp.dot(left, right, preferred_element_type=F32)


def pack_gram(gram):
    return jnp.concatenate([gram[8 * i : 8 * i + 8, :] for i in range(4)], axis=1)


def unpack_gram(packed):
    return jnp.concatenate([packed[:, K * i : K * i + K] for i in range(4)], axis=0)


def kernel(
    stamps, start, out,
    block, blockt, initial, panel, part1, got1, proj, gram_out, gram_core, gram_chip, gram_in, gram_all, sums, pair,
    sems, group_sems, core_sems, gram_sems, z_sems,
):
    s, p = lax.axis_index("samp"), lax.axis_index("pix")
    x, y, z, c = p // GY, p % GY, s // 2, s % 2

    def device(slot, core):
        dx, dy = OFFSETS[slot]
        return {"samp": z * 2 + core, "pix": ((x + dx) % GX) * GY + (y + dy) % GY}

    def at_z(dz):
        return {"samp": ((z + dz) % GZ) * 2 + c, "pix": p}

    other = 1 - c

    def send(src, dst, sem, to, arrived=None):
        pltpu.make_async_remote_copy(
            src_ref=src, dst_ref=dst, send_sem=sems.at[sem],
            recv_sem=sems.at[sem + 1] if arrived is None else arrived,
            device_id=to, device_id_type=MESH,
        ).start()

    def wait_on(ref, sem):
        pltpu.make_async_copy(ref, ref, sem).wait()

    def wait(ref, sem):
        wait_on(ref, sems.at[sem])

    barrier = pltpu.get_barrier_semaphore()
    for slot in FAR_FIRST:
        for core in range(2):
            pl.semaphore_signal(barrier, inc=1, device_id=device(slot, core), device_id_type=MESH)
    for dz in Z_STEPS:
        pl.semaphore_signal(barrier, inc=1, device_id=at_z(dz), device_id_type=MESH)
    pl.semaphore_signal(barrier, inc=1, device_id=device(0, other), device_id_type=MESH)
    pl.semaphore_wait(barrier, 2 * CHIPS - 1 + GZ - 1)

    def rows_of(slot):
        return block.at[pl.ds(pl.multiple_of(slot * 2 * ROWS + c * ROWS, ROWS), ROWS)]

    def pixels_of(to, core):
        return stamps.at[:, pl.ds(pl.multiple_of(to["pix"] * PC + core * PB, PB), PB)]

    def arrival(slot):
        return group_sems.at[GROUP_OF[slot]]

    for slot in FAR_FIRST:
        for core in range(2):
            to = device(slot, core)
            send(pixels_of(to, core), rows_of(BACK[slot]), 0, to, arrival(BACK[slot]))
    to = device(0, other)
    send(pixels_of(to, other), rows_of(0), 0, to, arrival(0))
    own = pltpu.make_async_copy(pixels_of(device(0, c), c), rows_of(0), sems.at[14])
    own.start()

    begin = pltpu.make_async_copy(start.at[:, pl.ds(pl.multiple_of(c * PB, PB), PB)], initial, sems.at[15])
    begin.start()

    def share_gram(turn, partial):
        gram_out[...] = pack_gram(partial)
        send(gram_out, gram_core.at[turn], 4, device(0, other), core_sems.at[turn])

    def share_chip_gram(turn):
        wait_on(gram_core.at[turn], core_sems.at[turn])
        gram_chip[...] = gram_out[...] + gram_core[turn]
        wait(gram_out, 4)
        for slot in FAR_FIRST:
            send(gram_chip, gram_in.at[turn, BACK[slot] - 1], 6, device(slot, c), gram_sems.at[turn])

    def sum_gram(turn):
        wait_on(gram_in.at[turn], gram_sems.at[turn])
        total = gram_chip[...]
        for i in range(CHIPS - 1):
            total = total + gram_in[turn, i]
        wait(gram_in.at[turn], 6)
        return unpack_gram(total)

    def gram_of(now):
        return lax.dot_general(now, now, NT, preferred_element_type=F32)

    def add_up_stamps(now, group):
        first, last = GROUPS[group]
        partial = jnp.dot(
            now, blockt[:, first * LANES : last * LANES], preferred_element_type=F32
        ).astype(BF)
        for i in range(last - first):
            for core in range(2):
                part1[first + i, core] = partial[HK * core : HK * core + HK, LANES * i : LANES * i + LANES]
        for slot in range(last - 1, first - 1, -1):
            if slot:
                for core in range(2):
                    send(part1.at[slot, core], got1.at[BACK[slot] * 2 - 1 + c], 2, device(slot, core))
            else:
                send(part1.at[0, other], got1.at[0], 2, device(0, other))

    def spread_stamps():
        wait(got1, 3)
        total = part1[0, c].astype(F32)
        for i in range(2 * CHIPS - 1):
            total = total + got1[i].astype(F32)
        proj[0, c] = total.astype(BF)
        for slot in FAR_FIRST:
            for core in range(2):
                send(proj.at[0, c], proj.at[BACK[slot], c], 8, device(slot, core), arrival(BACK[slot]))
        send(proj.at[0, c], proj.at[0, c], 8, device(0, other), arrival(0))
        wait(got1, 2)

    def add_up_pixels(turn):
        back = jnp.zeros((K, PB), F32)
        for group, (first, last) in enumerate(GROUPS):
            pieces = 2 * (last - first) - (first == 0)
            wait_on(got1.at[pl.ds(0, pieces)], arrival(first))
            raw = jnp.concatenate(
                [jnp.concatenate([proj[i, 0], proj[i, 1]], axis=0) for i in range(first, last)], axis=1
            )
            back = back + jnp.dot(
                raw, block[first * LANES : last * LANES, :], preferred_element_type=F32
            )
        sums[turn, z] = back.astype(BF)
        for dz in Z_STEPS:
            send(sums.at[turn, z], sums.at[turn, z], 10, at_z(dz), z_sems.at[turn])
        wait(got1, 8)

    def sum_pixels(turn):
        wait_on(sums.at[turn, pl.ds(0, GZ - 1)], z_sems.at[turn])
        wait(sums.at[turn, pl.ds(0, GZ - 1)], 10)
        total = sums[turn, 0].astype(F32)
        for i in range(1, GZ):
            total = total + sums[turn, i].astype(F32)
        return total

    begin.wait()
    own.wait()
    now = initial[...].astype(BF)
    for group in reversed(range(len(GROUPS))):
        first, last = GROUPS[group]
        remote = (last - first) * 2 * ROWS - (ROWS if first == 0 else 0)
        wait_on(block.at[pl.ds(0, remote)], arrival(first))
        blockt[:, first * LANES : last * LANES] = block[first * LANES : last * LANES, :].T
        add_up_stamps(now, group)
    wait(block.at[pl.ds(0, SB - ROWS)], 0)
    spread_stamps()
    add_up_pixels(0)
    panel[...] = sum_pixels(0).astype(BF)

    def sweep(step, carry):
        turn = lax.rem(step, 2)
        now = panel[...]
        for group in reversed(range(len(GROUPS))):
            add_up_stamps(now, group)
        share_gram(turn, gram_of(now))
        spread_stamps()
        share_chip_gram(turn)
        add_up_pixels(turn)
        factor = inverse_cholesky(sum_gram(turn))
        panel[...] = apply_factor(factor, sum_pixels(turn)).astype(BF)
        return carry

    lax.fori_loop(1, ITERS, sweep, 0)

    now = panel[...]
    send(panel, pair, 12, device(0, other))
    gram_all[0, c] = pack_gram(gram_of(now))
    for slot in FAR_FIRST:
        for core in range(2):
            send(gram_all.at[0, c], gram_all.at[BACK[slot], c], 6, device(slot, core))
    send(gram_all.at[0, c], gram_all.at[0, c], 6, device(0, other))
    wait(pair, 13)
    wait(pair, 12)
    wait(got1, 7)
    wait(got1, 6)
    total = gram_all[0, 0] + gram_all[0, 1]
    for slot in range(1, CHIPS):
        total = total + (gram_all[slot, 0] + gram_all[slot, 1])
    factor = inverse_cholesky(unpack_gram(total)) * SCALE
    out[:, pl.ds(pl.multiple_of(c * PB, PB), PB)] = apply_factor(factor, now.astype(F32))
    out[:, pl.ds(pl.multiple_of(other * PB, PB), PB)] = apply_factor(factor, pair[...].astype(F32))


def local(stamps, start_panel):
    vmem = pl.BlockSpec(memory_space=pltpu.VMEM)
    result = pl.pallas_call(
        kernel,
        out_shape=jax.ShapeDtypeStruct((K, PC), F32),
        in_specs=[pl.BlockSpec(memory_space=pl.ANY)] * 2,
        out_specs=vmem,
        scratch_shapes=[
            pltpu.VMEM((SB, PB), BF),
            pltpu.VMEM((PB, SB), BF),
            pltpu.VMEM((K, PB), F32),
            pltpu.VMEM((K, PB), BF),
            pltpu.VMEM((CHIPS, 2, HK, LANES), BF),
            pltpu.VMEM((2 * CHIPS - 1, HK, LANES), BF),
            pltpu.VMEM((CHIPS, 2, HK, LANES), BF),
            pltpu.VMEM((8, LANES), F32),
            pltpu.VMEM((2, 8, LANES), F32),
            pltpu.VMEM((8, LANES), F32),
            pltpu.VMEM((2, CHIPS - 1, 8, LANES), F32),
            pltpu.VMEM((CHIPS, 2, 8, LANES), F32),
            pltpu.VMEM((2, GZ, K, PB), BF),
            pltpu.VMEM((K, PB), BF),
            pltpu.SemaphoreType.DMA((16,)),
            pltpu.SemaphoreType.DMA((len(GROUPS),)),
            pltpu.SemaphoreType.DMA((2,)),
            pltpu.SemaphoreType.DMA((2,)),
            pltpu.SemaphoreType.DMA((2,)),
        ],
        compiler_params=pltpu.CompilerParams(
            collective_id=0, has_side_effects=True, vmem_limit_bytes=63 << 20
        ),
    )(stamps, start_panel.T)
    return result.T


def solution(mesh):
    return jax.shard_map(
        local,
        mesh=mesh,
        in_specs=(P(("samp", "pix"), None), P("pix", None)),
        out_specs=P("pix", None),
        check_vma=False,
    )
```

```python
import jax
import jax.numpy as jnp
from jax import lax
from jax.experimental import pallas as pl
from jax.experimental.pallas import tpu as pltpu
from jax.sharding import PartitionSpec as P

PIX = 16384
K = 32
ITERS = 10
SCALE = 128.0
GX, GY, GZ = 4, 4, 4
CHIPS = GX * GY
ROWS = 64
SB = CHIPS * 2 * ROWS
PC = PIX // CHIPS
PB = PC // 2
HK = K // 2
LANES = 128
TILES = PB // LANES
MESH = pl.DeviceIdType.MESH
NT = (((1,), (1,)), ((), ()))
BF, F32 = jnp.bfloat16, jnp.float32


def hops(offset):
    return sum(min(d, 4 - d) for d in offset)


def opposite(offset):
    return (offset[0] + GX // 2) % GX, (offset[1] + GY // 2) % GY


ALL = sorted(((dx, dy) for dx in range(GX) for dy in range(GY)), key=hops)
OFFSETS = []
for near in ALL:
    if near not in OFFSETS:
        OFFSETS += [near, opposite(near)]
BACK = [OFFSETS.index(((-dx) % GX, (-dy) % GY)) for dx, dy in OFFSETS]
HOPS = [hops(offset) for offset in OFFSETS]
FAR_FIRST = sorted(range(1, CHIPS), key=lambda slot: -HOPS[slot])
GROUPS = [(0, 4), (4, 10), (10, 16)]
GROUP_OF = [g for g, (first, last) in enumerate(GROUPS) for _ in range(first, last)]
Z_STEPS = [2, 1, 3]


def split3(a):
    hi = a.astype(BF)
    rest = a - hi.astype(F32)
    mid = rest.astype(BF)
    return hi, mid, (rest - mid.astype(F32)).astype(BF)


def inverse_cholesky(gram):
    rows = lax.broadcasted_iota(jnp.int32, (K, K), 0)
    cols = lax.broadcasted_iota(jnp.int32, (K, K), 1)
    work = jnp.concatenate([gram, jnp.where(rows == cols, 1.0, 0.0).astype(F32)], axis=1)
    below = lax.broadcasted_iota(jnp.int32, (K, 1), 0)
    for j in range(0, K, 2):
        one, two = work[j : j + 1, :], work[j + 1 : j + 2, :]
        pivot = lax.rsqrt(one[:, j : j + 1])
        under = two[:, j : j + 1] * pivot
        pivot2 = lax.rsqrt(two[:, j + 1 : j + 2] - under * under)
        row = one * pivot
        row2 = (two - under * row) * pivot2
        column = work[:, j : j + 1] * pivot
        column2 = (work[:, j + 1 : j + 2] - under * column) * pivot2
        rest = work - column * row - column2 * row2
        work = jnp.where(
            below > j + 1, rest, jnp.where(below == j, row, jnp.where(below == j + 1, row2, work))
        )
    return work[:, K:]


def apply_factor(factor, value):
    f, v = split3(factor), split3(value)
    pairs = [(0, 0), (0, 1), (1, 0), (1, 1), (0, 2), (2, 0)]
    left = jnp.concatenate([f[i] for i, _ in pairs], axis=1)
    right = jnp.concatenate([v[j] for _, j in pairs], axis=0)
    return jnp.dot(left, right, preferred_element_type=F32)


def pack_gram(gram):
    return jnp.concatenate([gram[8 * i : 8 * i + 8, :] for i in range(4)], axis=1)


def unpack_gram(packed):
    return jnp.concatenate([packed[:, K * i : K * i + K] for i in range(4)], axis=0)


def kernel(
    stamps, start, out,
    block, blockt, initial, panel, part1, got1, proj, gram_out, gram_core, gram_chip, gram_in, gram_all, sums, pair,
    sems, group_sems, got_sems, core_sems, gram_sems, z_sems,
):
    s, p = lax.axis_index("samp"), lax.axis_index("pix")
    x, y, z, c = p // GY, p % GY, s // 2, s % 2

    def device(slot, core):
        dx, dy = OFFSETS[slot]
        return {"samp": z * 2 + core, "pix": ((x + dx) % GX) * GY + (y + dy) % GY}

    def at_z(dz):
        return {"samp": ((z + dz) % GZ) * 2 + c, "pix": p}

    other = 1 - c

    def send(src, dst, sem, to, arrived=None):
        pltpu.make_async_remote_copy(
            src_ref=src, dst_ref=dst, send_sem=sems.at[sem],
            recv_sem=sems.at[sem + 1] if arrived is None else arrived,
            device_id=to, device_id_type=MESH,
        ).start()

    def wait_on(ref, sem):
        pltpu.make_async_copy(ref, ref, sem).wait()

    def wait(ref, sem):
        wait_on(ref, sems.at[sem])

    barrier = pltpu.get_barrier_semaphore()
    for slot in FAR_FIRST:
        for core in range(2):
            pl.semaphore_signal(barrier, inc=1, device_id=device(slot, core), device_id_type=MESH)
    for dz in Z_STEPS:
        pl.semaphore_signal(barrier, inc=1, device_id=at_z(dz), device_id_type=MESH)
    pl.semaphore_signal(barrier, inc=1, device_id=device(0, other), device_id_type=MESH)
    pl.semaphore_wait(barrier, 2 * CHIPS - 1 + GZ - 1)

    def rows_of(slot):
        return block.at[pl.ds(pl.multiple_of(slot * 2 * ROWS + c * ROWS, ROWS), ROWS)]

    def pixels_of(to, core):
        return stamps.at[:, pl.ds(pl.multiple_of(to["pix"] * PC + core * PB, PB), PB)]

    def arrival(slot):
        return group_sems.at[GROUP_OF[slot]]

    for slot in sorted(range(1, CHIPS), key=lambda slot: GROUP_OF[slot]):
        for core in range(2):
            to = device(slot, core)
            send(pixels_of(to, core), rows_of(BACK[slot]), 0, to, arrival(BACK[slot]))
    to = device(0, other)
    send(pixels_of(to, other), rows_of(0), 0, to, arrival(0))
    own = pltpu.make_async_copy(pixels_of(device(0, c), c), rows_of(0), sems.at[14])
    own.start()

    begin = pltpu.make_async_copy(start.at[:, pl.ds(pl.multiple_of(c * PB, PB), PB)], initial, sems.at[15])
    begin.start()

    def share_gram(turn, partial):
        gram_out[...] = pack_gram(partial)
        send(gram_out, gram_core.at[turn], 4, device(0, other), core_sems.at[turn])

    def share_chip_gram(turn):
        wait_on(gram_core.at[turn], core_sems.at[turn])
        gram_chip[...] = gram_out[...] + gram_core[turn]
        wait(gram_out, 4)
        for slot in FAR_FIRST:
            send(gram_chip, gram_in.at[turn, BACK[slot] - 1], 6, device(slot, c), gram_sems.at[turn])

    def sum_gram(turn):
        wait_on(gram_in.at[turn], gram_sems.at[turn])
        total = gram_chip[...]
        for i in range(CHIPS - 1):
            total = total + gram_in[turn, i]
        wait(gram_in.at[turn], 6)
        return unpack_gram(total)

    def gram_of(now):
        return lax.dot_general(now, now, NT, preferred_element_type=F32)

    def send_part(turn, slot, core):
        place = BACK[slot] * 2 - 1 + c if slot else 0
        send(part1.at[slot, core], got1.at[turn, place], 2, device(slot, core), got_sems.at[turn])

    def add_up_stamps(now, turn, group):
        first, last = GROUPS[group]
        partial = jnp.dot(
            now, blockt[:, first * LANES : last * LANES], preferred_element_type=F32
        ).astype(BF)
        for slot in range(first, last):
            for core in range(2):
                piece = partial[HK * core : HK * core + HK, LANES * (slot - first) : LANES * (slot - first + 1)]
                part1[slot, core, 0] = piece
                part1[slot ^ 1, core, 1] = piece
        for slot in FAR_FIRST:
            if first <= slot < last and HOPS[slot] > 1:
                for core in range(2):
                    send_part(turn, slot, core)

    def spread_stamps(turn):
        for slot in FAR_FIRST:
            if HOPS[slot] == 1:
                for core in range(2):
                    send_part(turn, slot, core)
        send_part(turn, 0, other)

    def gather_stamps(turn):
        wait_on(got1.at[turn], got_sems.at[turn])
        total = part1[0, c].astype(F32)
        for i in range(2 * CHIPS - 1):
            total = total + got1[turn, i].astype(F32)
        proj[0, c] = total[0].astype(BF)
        proj[1, c] = total[1].astype(BF)
        both = proj.at[pl.ds(0, 2), c]
        for slot in FAR_FIRST:
            for core in range(2):
                if HOPS[slot] == 2:
                    send(proj.at[0, c], proj.at[BACK[slot], c], 8, device(slot, core), arrival(BACK[slot]))
                elif HOPS[slot] == 1:
                    send(both, proj.at[pl.ds(BACK[slot], 2), c], 8, device(slot, core), arrival(BACK[slot]))
        send(both, both, 8, device(0, other), arrival(0))
        wait(got1.at[turn], 2)

    def add_up_pixels(turn):
        back = jnp.zeros((K, PB), F32)
        for first, last in GROUPS:
            tiles = 2 * (last - first) - (2 if first == 0 else 0)
            wait_on(got1.at[0, pl.ds(0, tiles // 2)], arrival(first))
            raw = jnp.concatenate(
                [jnp.concatenate([proj[i, 0], proj[i, 1]], axis=0) for i in range(first, last)], axis=1
            )
            back = back + jnp.dot(
                raw, block[first * LANES : last * LANES, :], preferred_element_type=F32
            )
        sums[turn, z] = back.astype(BF)
        for dz in Z_STEPS:
            send(sums.at[turn, z], sums.at[turn, z], 10, at_z(dz), z_sems.at[turn])
        wait(proj.at[pl.ds(0, CHIPS - 1)], 8)

    def sum_pixels(turn):
        wait_on(sums.at[turn, pl.ds(0, GZ - 1)], z_sems.at[turn])
        wait(sums.at[turn, pl.ds(0, GZ - 1)], 10)
        total = sums[turn, 0].astype(F32)
        for i in range(1, GZ):
            total = total + sums[turn, i].astype(F32)
        return total

    begin.wait()
    own.wait()
    now = initial[...].astype(BF)
    for group in range(len(GROUPS)):
        first, last = GROUPS[group]
        remote = (last - first) * 2 * ROWS - (ROWS if first == 0 else 0)
        wait_on(block.at[pl.ds(0, remote)], arrival(first))
        blockt[:, first * LANES : last * LANES] = block[first * LANES : last * LANES, :].T
        add_up_stamps(now, 0, group)
    spread_stamps(0)
    wait(block.at[pl.ds(0, SB - ROWS)], 0)
    gather_stamps(0)
    add_up_pixels(0)
    panel[...] = sum_pixels(0).astype(BF)

    def sweep(step, carry):
        turn = lax.rem(step, 2)
        now = panel[...]
        for group in range(len(GROUPS)):
            add_up_stamps(now, turn, group)
        spread_stamps(turn)
        share_gram(turn, gram_of(now))
        gather_stamps(turn)
        share_chip_gram(turn)
        add_up_pixels(turn)
        factor = inverse_cholesky(sum_gram(turn))
        panel[...] = apply_factor(factor, sum_pixels(turn)).astype(BF)
        return carry

    lax.fori_loop(1, ITERS, sweep, 0)

    now = panel[...]
    send(panel, pair, 12, device(0, other))
    gram_all[0, c] = pack_gram(gram_of(now))
    for slot in FAR_FIRST:
        for core in range(2):
            send(gram_all.at[0, c], gram_all.at[BACK[slot], c], 6, device(slot, core))
    send(gram_all.at[0, c], gram_all.at[0, c], 6, device(0, other))
    wait(pair, 13)
    wait(pair, 12)
    every = got1.at[0, :, 0]
    wait(every, 7)
    wait(every, 6)
    total = gram_all[0, 0] + gram_all[0, 1]
    for slot in range(1, CHIPS):
        total = total + (gram_all[slot, 0] + gram_all[slot, 1])
    factor = inverse_cholesky(unpack_gram(total)) * SCALE
    out[:, pl.ds(pl.multiple_of(c * PB, PB), PB)] = apply_factor(factor, now.astype(F32))
    out[:, pl.ds(pl.multiple_of(other * PB, PB), PB)] = apply_factor(factor, pair[...].astype(F32))


def local(stamps, start_panel):
    vmem = pl.BlockSpec(memory_space=pltpu.VMEM)
    result = pl.pallas_call(
        kernel,
        out_shape=jax.ShapeDtypeStruct((K, PC), F32),
        in_specs=[pl.BlockSpec(memory_space=pl.ANY)] * 2,
        out_specs=vmem,
        scratch_shapes=[
            pltpu.VMEM((SB, PB), BF),
            pltpu.VMEM((PB, SB), BF),
            pltpu.VMEM((K, PB), F32),
            pltpu.VMEM((K, PB), BF),
            pltpu.VMEM((CHIPS, 2, 2, HK, LANES), BF),
            pltpu.VMEM((2, 2 * CHIPS - 1, 2, HK, LANES), BF),
            pltpu.VMEM((CHIPS, 2, HK, LANES), BF),
            pltpu.VMEM((8, LANES), F32),
            pltpu.VMEM((2, 8, LANES), F32),
            pltpu.VMEM((8, LANES), F32),
            pltpu.VMEM((2, CHIPS - 1, 8, LANES), F32),
            pltpu.VMEM((CHIPS, 2, 8, LANES), F32),
            pltpu.VMEM((2, GZ, K, PB), BF),
            pltpu.VMEM((K, PB), BF),
            pltpu.SemaphoreType.DMA((16,)),
            pltpu.SemaphoreType.DMA((len(GROUPS),)),
            pltpu.SemaphoreType.DMA((2,)),
            pltpu.SemaphoreType.DMA((2,)),
            pltpu.SemaphoreType.DMA((2,)),
            pltpu.SemaphoreType.DMA((2,)),
        ],
        compiler_params=pltpu.CompilerParams(
            collective_id=0, has_side_effects=True, vmem_limit_bytes=63 << 20
        ),
    )(stamps, start_panel.T)
    return result.T


def solution(mesh):
    return jax.shard_map(
        local,
        mesh=mesh,
        in_specs=(P(("samp", "pix"), None), P("pix", None)),
        out_specs=P("pix", None),
        check_vma=False,
    )
```

```python
import jax
import jax.numpy as jnp
from jax import lax
from jax.experimental import pallas as pl
from jax.experimental.pallas import tpu as pltpu
from jax.sharding import PartitionSpec as P

PIX = 16384
K = 32
ITERS = 10
SCALE = 128.0
GX, GY, GZ = 4, 4, 4
CHIPS = GX * GY
ROWS = 64
SB = CHIPS * 2 * ROWS
PC = PIX // CHIPS
PB = PC // 2
HK = K // 2
LANES = 128
BLOCK = 4
TILES = PB // LANES
MESH = pl.DeviceIdType.MESH
NT = (((1,), (1,)), ((), ()))
BF, F32 = jnp.bfloat16, jnp.float32


def hops(offset):
    return sum(min(d, 4 - d) for d in offset)


def opposite(offset):
    return (offset[0] + GX // 2) % GX, (offset[1] + GY // 2) % GY


ALL = sorted(((dx, dy) for dx in range(GX) for dy in range(GY)), key=hops)
OFFSETS = []
for near in ALL:
    if near not in OFFSETS:
        OFFSETS += [near, opposite(near)]
BACK = [OFFSETS.index(((-dx) % GX, (-dy) % GY)) for dx, dy in OFFSETS]
HOPS = [hops(offset) for offset in OFFSETS]
FAR_FIRST = sorted(range(1, CHIPS), key=lambda slot: -HOPS[slot])
GROUPS = [(0, 4), (4, 12), (12, 16)]
GROUP_OF = [g for g, (first, last) in enumerate(GROUPS) for _ in range(first, last)]
Z_STEPS = [2, 1, 3]


def split3(a):
    hi = a.astype(BF)
    rest = a - hi.astype(F32)
    mid = rest.astype(BF)
    return hi, mid, (rest - mid.astype(F32)).astype(BF)


def inverse_cholesky(gram):
    rows = lax.broadcasted_iota(jnp.int32, (K, K), 0)
    cols = lax.broadcasted_iota(jnp.int32, (K, K), 1)
    work = jnp.concatenate([gram, jnp.where(rows == cols, 1.0, 0.0).astype(F32)], axis=1)
    place = lax.broadcasted_iota(jnp.int32, (K, 2 * K), 0)
    for j in range(0, K, BLOCK):
        columns = [jnp.broadcast_to(work[:, j + t : j + t + 1], (K, 2 * K)) for t in range(BLOCK)]
        rows = [work[j + t : j + t + 1, :] for t in range(BLOCK)]
        for t in range(BLOCK):
            pivot = lax.rsqrt(columns[t][j + t : j + t + 1, :])
            rows[t] = rows[t] * pivot
            columns[t] = columns[t] * pivot
            for u in range(t + 1, BLOCK):
                factor = columns[t][j + u : j + u + 1, :]
                rows[u] = rows[u] - factor * rows[t]
                columns[u] = columns[u] - columns[t] * factor
        rest = work
        for t in range(BLOCK):
            rest = rest - columns[t] * rows[t]
        for t in range(BLOCK):
            work = jnp.where(place == j + t, rows[t], work)
        work = jnp.where(place >= j + BLOCK, rest, work)
    return work[:, K:]


def apply_factor(factor, value):
    f, v = split3(factor), split3(value)
    pairs = [(0, 0), (0, 1), (1, 0), (1, 1), (0, 2), (2, 0)]
    left = jnp.concatenate([f[i] for i, _ in pairs], axis=1)
    right = jnp.concatenate([v[j] for _, j in pairs], axis=0)
    return jnp.dot(left, right, preferred_element_type=F32)


def pack_gram(gram):
    return jnp.concatenate([gram[8 * i : 8 * i + 8, :] for i in range(4)], axis=1)


def unpack_gram(packed):
    return jnp.concatenate([packed[:, K * i : K * i + K] for i in range(4)], axis=0)


def kernel(
    stamps, start, out,
    block, blockt, initial, panel, part1, got1, proj, gram_out, gram_core, gram_chip, gram_in, gram_all, sums, pair,
    sems, group_sems, got_sems, core_sems, gram_sems, z_sems,
):
    s, p = lax.axis_index("samp"), lax.axis_index("pix")
    x, y, z, c = p // GY, p % GY, s // 2, s % 2

    def device(slot, core):
        dx, dy = OFFSETS[slot]
        return {"samp": z * 2 + core, "pix": ((x + dx) % GX) * GY + (y + dy) % GY}

    def at_z(dz):
        return {"samp": ((z + dz) % GZ) * 2 + c, "pix": p}

    other = 1 - c

    def send(src, dst, sem, to, arrived=None):
        pltpu.make_async_remote_copy(
            src_ref=src, dst_ref=dst, send_sem=sems.at[sem],
            recv_sem=sems.at[sem + 1] if arrived is None else arrived,
            device_id=to, device_id_type=MESH,
        ).start()

    def wait_on(ref, sem):
        pltpu.make_async_copy(ref, ref, sem).wait()

    def wait(ref, sem):
        wait_on(ref, sems.at[sem])

    barrier = pltpu.get_barrier_semaphore()
    for slot in FAR_FIRST:
        for core in range(2):
            pl.semaphore_signal(barrier, inc=1, device_id=device(slot, core), device_id_type=MESH)
    for dz in Z_STEPS:
        pl.semaphore_signal(barrier, inc=1, device_id=at_z(dz), device_id_type=MESH)
    pl.semaphore_signal(barrier, inc=1, device_id=device(0, other), device_id_type=MESH)
    pl.semaphore_wait(barrier, 2 * CHIPS - 1 + GZ - 1)

    def rows_of(slot):
        return block.at[pl.ds(pl.multiple_of(slot * 2 * ROWS + c * ROWS, ROWS), ROWS)]

    def pixels_of(to, core):
        return stamps.at[:, pl.ds(pl.multiple_of(to["pix"] * PC + core * PB, PB), PB)]

    def arrival(slot):
        return group_sems.at[GROUP_OF[slot]]

    for slot in sorted(range(1, CHIPS), key=lambda slot: GROUP_OF[slot]):
        for core in range(2):
            to = device(slot, core)
            send(pixels_of(to, core), rows_of(BACK[slot]), 0, to, arrival(BACK[slot]))
    to = device(0, other)
    send(pixels_of(to, other), rows_of(0), 0, to, arrival(0))
    own = pltpu.make_async_copy(pixels_of(device(0, c), c), rows_of(0), sems.at[14])
    own.start()

    begin = pltpu.make_async_copy(start.at[:, pl.ds(pl.multiple_of(c * PB, PB), PB)], initial, sems.at[15])
    begin.start()

    def share_gram(turn, partial):
        gram_out[...] = pack_gram(partial)
        send(gram_out, gram_core.at[turn], 4, device(0, other), core_sems.at[turn])

    def share_chip_gram(turn):
        wait_on(gram_core.at[turn], core_sems.at[turn])
        gram_chip[...] = gram_out[...] + gram_core[turn]
        wait(gram_out, 4)
        for slot in FAR_FIRST:
            send(gram_chip, gram_in.at[turn, BACK[slot] - 1], 6, device(slot, c), gram_sems.at[turn])

    def sum_gram(turn):
        wait_on(gram_in.at[turn], gram_sems.at[turn])
        total = gram_chip[...]
        for i in range(CHIPS - 1):
            total = total + gram_in[turn, i]
        wait(gram_in.at[turn], 6)
        return unpack_gram(total)

    def gram_of(now):
        return lax.dot_general(now, now, NT, preferred_element_type=F32)

    def send_part(turn, slot, core):
        place = BACK[slot] * 2 - 1 + c if slot else 0
        send(part1.at[slot, core], got1.at[turn, place], 2, device(slot, core), got_sems.at[turn])

    def add_up_stamps(now, turn, group, least):
        first, last = GROUPS[group]
        partial = jnp.dot(
            now, blockt[:, first * LANES : last * LANES], preferred_element_type=F32
        ).astype(BF)
        for slot in range(first, last):
            for core in range(2):
                piece = partial[HK * core : HK * core + HK, LANES * (slot - first) : LANES * (slot - first + 1)]
                part1[slot, core, 0] = piece
                part1[slot ^ 1, core, 1] = piece
        for slot in FAR_FIRST:
            if first <= slot < last and HOPS[slot] >= least:
                for core in range(2):
                    send_part(turn, slot, core)

    def add_up_nearest(turn):
        for slot in FAR_FIRST:
            if HOPS[slot] == 1:
                for core in range(2):
                    send_part(turn, slot, core)
        send_part(turn, 0, other)

    def gather_stamps(turn):
        wait_on(got1.at[turn], got_sems.at[turn])
        total = part1[0, c].astype(F32)
        for i in range(2 * CHIPS - 1):
            total = total + got1[turn, i].astype(F32)
        proj[0, c] = total[0].astype(BF)
        proj[1, c] = total[1].astype(BF)
        both = proj.at[pl.ds(0, 2), c]
        for slot in FAR_FIRST:
            for core in range(2):
                if HOPS[slot] == 2:
                    send(proj.at[0, c], proj.at[BACK[slot], c], 8, device(slot, core), arrival(BACK[slot]))
                elif HOPS[slot] == 1:
                    send(both, proj.at[pl.ds(BACK[slot], 2), c], 8, device(slot, core), arrival(BACK[slot]))
        send(both, both, 8, device(0, other), arrival(0))
        wait(got1.at[turn], 2)

    def add_up_pixels(turn):
        back = jnp.zeros((K, PB), F32)
        for first, last in GROUPS:
            tiles = 2 * (last - first) - (2 if first == 0 else 0)
            wait_on(got1.at[0, pl.ds(0, tiles // 2)], arrival(first))
            raw = jnp.concatenate(
                [jnp.concatenate([proj[i, 0], proj[i, 1]], axis=0) for i in range(first, last)], axis=1
            )
            back = back + jnp.dot(
                raw, block[first * LANES : last * LANES, :], preferred_element_type=F32
            )
        sums[turn, z] = back.astype(BF)
        for dz in Z_STEPS:
            send(sums.at[turn, z], sums.at[turn, z], 10, at_z(dz), z_sems.at[turn])
        wait(proj.at[pl.ds(0, CHIPS - 1)], 8)

    def sum_pixels(turn):
        wait_on(sums.at[turn, pl.ds(0, GZ - 1)], z_sems.at[turn])
        wait(sums.at[turn, pl.ds(0, GZ - 1)], 10)
        total = sums[turn, 0].astype(F32)
        for i in range(1, GZ):
            total = total + sums[turn, i].astype(F32)
        return total

    begin.wait()
    own.wait()
    now = initial[...].astype(BF)
    for group in range(len(GROUPS)):
        first, last = GROUPS[group]
        remote = (last - first) * 2 * ROWS - (ROWS if first == 0 else 0)
        wait_on(block.at[pl.ds(0, remote)], arrival(first))
        blockt[:, first * LANES : last * LANES] = block[first * LANES : last * LANES, :].T
        add_up_stamps(now, 0, group, 1)
        if first == 0:
            send_part(0, 0, other)
    wait(block.at[pl.ds(0, SB - ROWS)], 0)
    gather_stamps(0)
    add_up_pixels(0)

    def sweep(step, now):
        turn = lax.rem(step, 2)
        for group in range(len(GROUPS)):
            add_up_stamps(now, turn, group, 2)
        add_up_nearest(turn)
        share_gram(turn, gram_of(now))
        gather_stamps(turn)
        share_chip_gram(turn)
        add_up_pixels(turn)
        factor = inverse_cholesky(sum_gram(turn))
        return apply_factor(factor, sum_pixels(turn)).astype(BF)

    now = lax.fori_loop(1, ITERS, sweep, sum_pixels(0).astype(BF))

    panel[...] = now
    send(panel, pair, 12, device(0, other))
    gram_all[0, c] = pack_gram(gram_of(now))
    for slot in FAR_FIRST:
        for core in range(2):
            send(gram_all.at[0, c], gram_all.at[BACK[slot], c], 6, device(slot, core))
    send(gram_all.at[0, c], gram_all.at[0, c], 6, device(0, other))
    wait(pair, 13)
    wait(pair, 12)
    every = got1.at[0, :, 0]
    wait(every, 7)
    wait(every, 6)
    total = gram_all[0, 0] + gram_all[0, 1]
    for slot in range(1, CHIPS):
        total = total + (gram_all[slot, 0] + gram_all[slot, 1])
    factor = inverse_cholesky(unpack_gram(total)) * SCALE
    out[:, pl.ds(pl.multiple_of(c * PB, PB), PB)] = apply_factor(factor, now.astype(F32))
    out[:, pl.ds(pl.multiple_of(other * PB, PB), PB)] = apply_factor(factor, pair[...].astype(F32))


def local(stamps, start_panel):
    vmem = pl.BlockSpec(memory_space=pltpu.VMEM)
    result = pl.pallas_call(
        kernel,
        out_shape=jax.ShapeDtypeStruct((K, PC), F32),
        in_specs=[pl.BlockSpec(memory_space=pl.ANY)] * 2,
        out_specs=vmem,
        scratch_shapes=[
            pltpu.VMEM((SB, PB), BF),
            pltpu.VMEM((PB, SB), BF),
            pltpu.VMEM((K, PB), F32),
            pltpu.VMEM((K, PB), BF),
            pltpu.VMEM((CHIPS, 2, 2, HK, LANES), BF),
            pltpu.VMEM((2, 2 * CHIPS - 1, 2, HK, LANES), BF),
            pltpu.VMEM((CHIPS, 2, HK, LANES), BF),
            pltpu.VMEM((8, LANES), F32),
            pltpu.VMEM((2, 8, LANES), F32),
            pltpu.VMEM((8, LANES), F32),
            pltpu.VMEM((2, CHIPS - 1, 8, LANES), F32),
            pltpu.VMEM((CHIPS, 2, 8, LANES), F32),
            pltpu.VMEM((2, GZ, K, PB), BF),
            pltpu.VMEM((K, PB), BF),
            pltpu.SemaphoreType.DMA((16,)),
            pltpu.SemaphoreType.DMA((len(GROUPS),)),
            pltpu.SemaphoreType.DMA((2,)),
            pltpu.SemaphoreType.DMA((2,)),
            pltpu.SemaphoreType.DMA((2,)),
            pltpu.SemaphoreType.DMA((2,)),
        ],
        compiler_params=pltpu.CompilerParams(
            collective_id=0, has_side_effects=True, vmem_limit_bytes=63 << 20
        ),
    )(stamps, start_panel.T)
    return result.T


def solution(mesh):
    return jax.shard_map(
        local,
        mesh=mesh,
        in_specs=(P(("samp", "pix"), None), P("pix", None)),
        out_specs=P("pix", None),
        check_vma=False,
    )
```

```python
import jax
import jax.numpy as jnp
from jax import lax
from jax.experimental import pallas as pl
from jax.experimental.pallas import tpu as pltpu
from jax.sharding import PartitionSpec as P

PIX = 16384
K = 32
ITERS = 10
SCALE = 128.0
GX, GY, GZ = 4, 4, 4
CHIPS = GX * GY
ROWS = 64
SB = CHIPS * 2 * ROWS
PC = PIX // CHIPS
PB = PC // 2
HK = K // 2
LANES = 128
BLOCK = 4
TILES = PB // LANES
MESH = pl.DeviceIdType.MESH
NT = (((1,), (1,)), ((), ()))
BF, F32 = jnp.bfloat16, jnp.float32


def hops(offset):
    return sum(min(d, 4 - d) for d in offset)


def opposite(offset):
    return (offset[0] + GX // 2) % GX, (offset[1] + GY // 2) % GY


ALL = sorted(((dx, dy) for dx in range(GX) for dy in range(GY)), key=hops)
OFFSETS = []
for near in ALL:
    if near not in OFFSETS:
        OFFSETS += [near, opposite(near)]
BACK = [OFFSETS.index(((-dx) % GX, (-dy) % GY)) for dx, dy in OFFSETS]
HOPS = [hops(offset) for offset in OFFSETS]
FAR_FIRST = sorted(range(1, CHIPS), key=lambda slot: -HOPS[slot])
GROUPS = [(0, 2), (2, 6), (6, 10), (10, 14), (14, 16)]
PUSH = [(0, 2), (2, 10), (10, 14), (14, 16)]
GROUP_OF = [g for g, (first, last) in enumerate(GROUPS) for _ in range(first, last)]
Z_STEPS = [2, 1, 3]


def split3(a):
    hi = a.astype(BF)
    rest = a - hi.astype(F32)
    mid = rest.astype(BF)
    return hi, mid, (rest - mid.astype(F32)).astype(BF)


def inverse_cholesky(gram):
    rows = lax.broadcasted_iota(jnp.int32, (K, K), 0)
    cols = lax.broadcasted_iota(jnp.int32, (K, K), 1)
    work = jnp.concatenate([gram, jnp.where(rows == cols, 1.0, 0.0).astype(F32)], axis=1)
    place = lax.broadcasted_iota(jnp.int32, (K, 2 * K), 0)
    for j in range(0, K, BLOCK):
        columns = [jnp.broadcast_to(work[:, j + t : j + t + 1], (K, 2 * K)) for t in range(BLOCK)]
        rows = [work[j + t : j + t + 1, :] for t in range(BLOCK)]
        for t in range(BLOCK):
            pivot = lax.rsqrt(columns[t][j + t : j + t + 1, :])
            rows[t] = rows[t] * pivot
            columns[t] = columns[t] * pivot
            for u in range(t + 1, BLOCK):
                factor = columns[t][j + u : j + u + 1, :]
                rows[u] = rows[u] - factor * rows[t]
                columns[u] = columns[u] - columns[t] * factor
        rest = work
        for t in range(BLOCK):
            rest = rest - columns[t] * rows[t]
        for t in range(BLOCK):
            work = jnp.where(place == j + t, rows[t], work)
        work = jnp.where(place >= j + BLOCK, rest, work)
    return work[:, K:]


def apply_factor(factor, value):
    f, v = split3(factor), split3(value)
    pairs = [(0, 0), (0, 1), (1, 0), (1, 1), (0, 2), (2, 0)]
    left = jnp.concatenate([f[i] for i, _ in pairs], axis=1)
    right = jnp.concatenate([v[j] for _, j in pairs], axis=0)
    return jnp.dot(left, right, preferred_element_type=F32)


def pack_gram(gram):
    return jnp.concatenate([gram[8 * i : 8 * i + 8, :] for i in range(4)], axis=1)


def unpack_gram(packed):
    return jnp.concatenate([packed[:, K * i : K * i + K] for i in range(4)], axis=0)


def kernel(
    stamps, start, out,
    block, blockt, initial, panel, part1, got1, proj, gram_out, gram_core, gram_chip, gram_in, gram_all, sums, pair,
    sems, group_sems, got_sems, core_sems, gram_sems, z_sems,
):
    s, p = lax.axis_index("samp"), lax.axis_index("pix")
    x, y, z, c = p // GY, p % GY, s // 2, s % 2

    def device(slot, core):
        dx, dy = OFFSETS[slot]
        return {"samp": z * 2 + core, "pix": ((x + dx) % GX) * GY + (y + dy) % GY}

    def at_z(dz):
        return {"samp": ((z + dz) % GZ) * 2 + c, "pix": p}

    other = 1 - c

    def send(src, dst, sem, to, arrived=None):
        pltpu.make_async_remote_copy(
            src_ref=src, dst_ref=dst, send_sem=sems.at[sem],
            recv_sem=sems.at[sem + 1] if arrived is None else arrived,
            device_id=to, device_id_type=MESH,
        ).start()

    def wait_on(ref, sem):
        pltpu.make_async_copy(ref, ref, sem).wait()

    def wait(ref, sem):
        wait_on(ref, sems.at[sem])

    barrier = pltpu.get_barrier_semaphore()
    for slot in FAR_FIRST:
        for core in range(2):
            pl.semaphore_signal(barrier, inc=1, device_id=device(slot, core), device_id_type=MESH)
    for dz in Z_STEPS:
        pl.semaphore_signal(barrier, inc=1, device_id=at_z(dz), device_id_type=MESH)
    pl.semaphore_signal(barrier, inc=1, device_id=device(0, other), device_id_type=MESH)
    pl.semaphore_wait(barrier, 2 * CHIPS - 1 + GZ - 1)

    def rows_of(slot):
        return block.at[pl.ds(pl.multiple_of(slot * 2 * ROWS + c * ROWS, ROWS), ROWS)]

    def pixels_of(to, core):
        return stamps.at[:, pl.ds(pl.multiple_of(to["pix"] * PC + core * PB, PB), PB)]

    def arrival(slot):
        return group_sems.at[GROUP_OF[slot]]

    for slot in sorted(range(1, CHIPS), key=lambda slot: GROUP_OF[slot]):
        for core in range(2):
            to = device(slot, core)
            send(pixels_of(to, core), rows_of(BACK[slot]), 0, to, arrival(BACK[slot]))
    to = device(0, other)
    send(pixels_of(to, other), rows_of(0), 0, to, arrival(0))
    own = pltpu.make_async_copy(pixels_of(device(0, c), c), rows_of(0), sems.at[14])
    own.start()

    begin = pltpu.make_async_copy(start.at[:, pl.ds(pl.multiple_of(c * PB, PB), PB)], initial, sems.at[15])
    begin.start()

    def share_gram(turn, partial):
        gram_out[...] = pack_gram(partial)
        send(gram_out, gram_core.at[turn], 4, device(0, other), core_sems.at[turn])

    def share_chip_gram(turn):
        wait_on(gram_core.at[turn], core_sems.at[turn])
        gram_chip[...] = gram_out[...] + gram_core[turn]
        wait(gram_out, 4)
        for slot in FAR_FIRST:
            send(gram_chip, gram_in.at[turn, BACK[slot] - 1], 6, device(slot, c), gram_sems.at[turn])

    def sum_gram(turn):
        wait_on(gram_in.at[turn], gram_sems.at[turn])
        total = gram_chip[...]
        for i in range(CHIPS - 1):
            total = total + gram_in[turn, i]
        wait(gram_in.at[turn], 6)
        return unpack_gram(total)

    def gram_of(now):
        return lax.dot_general(now, now, NT, preferred_element_type=F32)

    def send_part(turn, slot, core):
        place = BACK[slot] * 2 - 1 + c if slot else 0
        send(part1.at[slot, core], got1.at[turn, place], 2, device(slot, core), got_sems.at[turn])

    def add_up_stamps(now, turn, group, least):
        first, last = group
        partial = jnp.dot(
            now, blockt[:, first * LANES : last * LANES], preferred_element_type=F32
        ).astype(BF)
        for slot in range(first, last):
            for core in range(2):
                piece = partial[HK * core : HK * core + HK, LANES * (slot - first) : LANES * (slot - first + 1)]
                part1[slot, core, 0] = piece
                part1[slot ^ 1, core, 1] = piece
        for slot in FAR_FIRST:
            if first <= slot < last and HOPS[slot] >= least:
                for core in range(2):
                    send_part(turn, slot, core)

    def add_up_nearest(turn):
        for slot in FAR_FIRST:
            if HOPS[slot] == 1:
                for core in range(2):
                    send_part(turn, slot, core)
        send_part(turn, 0, other)

    def gather_stamps(turn):
        wait_on(got1.at[turn], got_sems.at[turn])
        total = part1[0, c].astype(F32)
        for i in range(2 * CHIPS - 1):
            total = total + got1[turn, i].astype(F32)
        proj[0, c] = total[0].astype(BF)
        proj[1, c] = total[1].astype(BF)
        both = proj.at[pl.ds(0, 2), c]
        for slot in FAR_FIRST:
            for core in range(2):
                if HOPS[slot] == 2:
                    send(proj.at[0, c], proj.at[BACK[slot], c], 8, device(slot, core), arrival(BACK[slot]))
                elif HOPS[slot] == 1:
                    send(both, proj.at[pl.ds(BACK[slot], 2), c], 8, device(slot, core), arrival(BACK[slot]))
        send(both, both, 8, device(0, other), arrival(0))
        wait(got1.at[turn], 2)

    def add_up_pixels(turn, then=None):
        back = jnp.zeros((K, PB), F32)
        for first, last in GROUPS:
            tiles = 2 * (last - first) - (2 if first == 0 else 0)
            wait_on(got1.at[0, pl.ds(0, tiles // 2)], arrival(first))
            if first == 0 and then is not None:
                then(turn)
            raw = jnp.concatenate(
                [jnp.concatenate([proj[i, 0], proj[i, 1]], axis=0) for i in range(first, last)], axis=1
            )
            back = back + jnp.dot(
                raw, block[first * LANES : last * LANES, :], preferred_element_type=F32
            )
        sums[turn, z] = back.astype(BF)
        for dz in Z_STEPS:
            send(sums.at[turn, z], sums.at[turn, z], 10, at_z(dz), z_sems.at[turn])
        wait(proj.at[pl.ds(0, CHIPS - 1)], 8)

    def sum_pixels(turn):
        wait_on(sums.at[turn, pl.ds(0, GZ - 1)], z_sems.at[turn])
        wait(sums.at[turn, pl.ds(0, GZ - 1)], 10)
        total = sums[turn, 0].astype(F32)
        for i in range(1, GZ):
            total = total + sums[turn, i].astype(F32)
        return total

    begin.wait()
    own.wait()
    now = initial[...].astype(BF)
    for group in range(len(GROUPS)):
        first, last = GROUPS[group]
        remote = (last - first) * 2 * ROWS - (ROWS if first == 0 else 0)
        wait_on(block.at[pl.ds(0, remote)], arrival(first))
        blockt[:, first * LANES : last * LANES] = block[first * LANES : last * LANES, :].T
        add_up_stamps(now, 0, GROUPS[group], 1)
        if first == 0:
            send_part(0, 0, other)
    wait(block.at[pl.ds(0, SB - ROWS)], 0)
    gather_stamps(0)
    add_up_pixels(0)

    def sweep(step, now):
        turn = lax.rem(step, 2)
        for group in PUSH:
            add_up_stamps(now, turn, group, 2)
        add_up_nearest(turn)
        share_gram(turn, gram_of(now))
        gather_stamps(turn)
        add_up_pixels(turn, share_chip_gram)
        factor = inverse_cholesky(sum_gram(turn))
        return apply_factor(factor, sum_pixels(turn)).astype(BF)

    now = lax.fori_loop(1, ITERS, sweep, sum_pixels(0).astype(BF))

    panel[...] = now
    send(panel, pair, 12, device(0, other))
    gram_all[0, c] = pack_gram(gram_of(now))
    for slot in FAR_FIRST:
        for core in range(2):
            send(gram_all.at[0, c], gram_all.at[BACK[slot], c], 6, device(slot, core))
    send(gram_all.at[0, c], gram_all.at[0, c], 6, device(0, other))
    wait(pair, 13)
    wait(pair, 12)
    every = got1.at[0, :, 0]
    wait(every, 7)
    wait(every, 6)
    total = gram_all[0, 0] + gram_all[0, 1]
    for slot in range(1, CHIPS):
        total = total + (gram_all[slot, 0] + gram_all[slot, 1])
    factor = inverse_cholesky(unpack_gram(total)) * SCALE
    out[:, pl.ds(pl.multiple_of(c * PB, PB), PB)] = apply_factor(factor, now.astype(F32))
    out[:, pl.ds(pl.multiple_of(other * PB, PB), PB)] = apply_factor(factor, pair[...].astype(F32))


def local(stamps, start_panel):
    vmem = pl.BlockSpec(memory_space=pltpu.VMEM)
    result = pl.pallas_call(
        kernel,
        out_shape=jax.ShapeDtypeStruct((K, PC), F32),
        in_specs=[pl.BlockSpec(memory_space=pl.ANY)] * 2,
        out_specs=vmem,
        scratch_shapes=[
            pltpu.VMEM((SB, PB), BF),
            pltpu.VMEM((PB, SB), BF),
            pltpu.VMEM((K, PB), F32),
            pltpu.VMEM((K, PB), BF),
            pltpu.VMEM((CHIPS, 2, 2, HK, LANES), BF),
            pltpu.VMEM((2, 2 * CHIPS - 1, 2, HK, LANES), BF),
            pltpu.VMEM((CHIPS, 2, HK, LANES), BF),
            pltpu.VMEM((8, LANES), F32),
            pltpu.VMEM((2, 8, LANES), F32),
            pltpu.VMEM((8, LANES), F32),
            pltpu.VMEM((2, CHIPS - 1, 8, LANES), F32),
            pltpu.VMEM((CHIPS, 2, 8, LANES), F32),
            pltpu.VMEM((2, GZ, K, PB), BF),
            pltpu.VMEM((K, PB), BF),
            pltpu.SemaphoreType.DMA((16,)),
            pltpu.SemaphoreType.DMA((len(GROUPS),)),
            pltpu.SemaphoreType.DMA((2,)),
            pltpu.SemaphoreType.DMA((2,)),
            pltpu.SemaphoreType.DMA((2,)),
            pltpu.SemaphoreType.DMA((2,)),
        ],
        compiler_params=pltpu.CompilerParams(
            collective_id=0, has_side_effects=True, vmem_limit_bytes=63 << 20
        ),
    )(stamps, start_panel.T)
    return result.T


def solution(mesh):
    return jax.shard_map(
        local,
        mesh=mesh,
        in_specs=(P(("samp", "pix"), None), P("pix", None)),
        out_specs=P("pix", None),
        check_vma=False,
    )
```

```python
import jax
import jax.numpy as jnp
from jax import lax
from jax.experimental import pallas as pl
from jax.experimental.pallas import tpu as pltpu
from jax.sharding import PartitionSpec as P

PIX = 16384
K = 32
ITERS = 10
SCALE = 128.0
GX, GY, GZ = 4, 4, 4
CHIPS = GX * GY
ROWS = 64
SB = CHIPS * 2 * ROWS
PC = PIX // CHIPS
PB = PC // 2
HK = K // 2
LANES = 128
BLOCK = 4
TILES = PB // LANES
MESH = pl.DeviceIdType.MESH
NT = (((1,), (1,)), ((), ()))
BF, F32 = jnp.bfloat16, jnp.float32


def hops(offset):
    return sum(min(d, 4 - d) for d in offset)


def opposite(offset):
    return (offset[0] + GX // 2) % GX, (offset[1] + GY // 2) % GY


ALL = sorted(((dx, dy) for dx in range(GX) for dy in range(GY)), key=hops)
OFFSETS = []
for near in ALL:
    if near not in OFFSETS:
        OFFSETS += [near, opposite(near)]
BACK = [OFFSETS.index(((-dx) % GX, (-dy) % GY)) for dx, dy in OFFSETS]
HOPS = [hops(offset) for offset in OFFSETS]
FAR_FIRST = sorted(range(1, CHIPS), key=lambda slot: -HOPS[slot])
GROUPS = [(0, 2), (2, 6), (6, 10), (10, 14), (14, 16)]
PUSH = [(0, 2), (2, 10), (10, 14), (14, 16)]
GROUP_OF = [g for g, (first, last) in enumerate(GROUPS) for _ in range(first, last)]
Z_STEPS = [2, 1, 3]


def split3(a):
    hi = a.astype(BF)
    rest = a - hi.astype(F32)
    mid = rest.astype(BF)
    return hi, mid, (rest - mid.astype(F32)).astype(BF)


def inverse_cholesky(gram):
    rows = lax.broadcasted_iota(jnp.int32, (K, K), 0)
    cols = lax.broadcasted_iota(jnp.int32, (K, K), 1)
    work = jnp.concatenate([gram, jnp.where(rows == cols, 1.0, 0.0).astype(F32)], axis=1)
    place = lax.broadcasted_iota(jnp.int32, (K, 2 * K), 0)
    for j in range(0, K, BLOCK):
        columns = [jnp.broadcast_to(work[:, j + t : j + t + 1], (K, 2 * K)) for t in range(BLOCK)]
        rows = [work[j + t : j + t + 1, :] for t in range(BLOCK)]
        for t in range(BLOCK):
            pivot = lax.rsqrt(columns[t][j + t : j + t + 1, :])
            rows[t] = rows[t] * pivot
            columns[t] = columns[t] * pivot
            for u in range(t + 1, BLOCK):
                factor = columns[t][j + u : j + u + 1, :]
                rows[u] = rows[u] - factor * rows[t]
                columns[u] = columns[u] - columns[t] * factor
        rest = work
        for t in range(BLOCK):
            rest = rest - columns[t] * rows[t]
        for t in range(BLOCK):
            work = jnp.where(place == j + t, rows[t], work)
        work = jnp.where(place >= j + BLOCK, rest, work)
    return work[:, K:]


def apply_factor(factor, value):
    f, v = split3(factor), split3(value)
    pairs = [(0, 0), (0, 1), (1, 0), (1, 1), (0, 2), (2, 0)]
    left = jnp.concatenate([f[i] for i, _ in pairs], axis=1)
    right = jnp.concatenate([v[j] for _, j in pairs], axis=0)
    return jnp.dot(left, right, preferred_element_type=F32)


def pack_gram(gram):
    return jnp.concatenate([gram[8 * i : 8 * i + 8, :] for i in range(4)], axis=1)


def unpack_gram(packed):
    return jnp.concatenate([packed[:, K * i : K * i + K] for i in range(4)], axis=0)


def kernel(
    stamps, start, out,
    block, blockt, initial, panel, part1, got1, proj, gram_out, gram_core, gram_chip, gram_in, gram_all, sums, pair,
    sems, group_sems, got_sems, core_sems, gram_sems, z_sems,
):
    s, p = lax.axis_index("samp"), lax.axis_index("pix")
    x, y, z, c = p // GY, p % GY, s // 2, s % 2

    def device(slot, core):
        dx, dy = OFFSETS[slot]
        return {"samp": z * 2 + core, "pix": ((x + dx) % GX) * GY + (y + dy) % GY}

    def at_z(dz):
        return {"samp": ((z + dz) % GZ) * 2 + c, "pix": p}

    other = 1 - c

    def send(src, dst, sem, to, arrived=None):
        pltpu.make_async_remote_copy(
            src_ref=src, dst_ref=dst, send_sem=sems.at[sem],
            recv_sem=sems.at[sem + 1] if arrived is None else arrived,
            device_id=to, device_id_type=MESH,
        ).start()

    def wait_on(ref, sem):
        pltpu.make_async_copy(ref, ref, sem).wait()

    def wait(ref, sem):
        wait_on(ref, sems.at[sem])

    barrier = pltpu.get_barrier_semaphore()
    for slot in FAR_FIRST:
        for core in range(2):
            pl.semaphore_signal(barrier, inc=1, device_id=device(slot, core), device_id_type=MESH)
    for dz in Z_STEPS:
        pl.semaphore_signal(barrier, inc=1, device_id=at_z(dz), device_id_type=MESH)
    pl.semaphore_signal(barrier, inc=1, device_id=device(0, other), device_id_type=MESH)
    pl.semaphore_wait(barrier, 2 * CHIPS - 1 + GZ - 1)

    def rows_of(slot):
        return block.at[pl.ds(pl.multiple_of(slot * 2 * ROWS + c * ROWS, ROWS), ROWS)]

    def pixels_of(to, core):
        return stamps.at[:, pl.ds(pl.multiple_of(to["pix"] * PC + core * PB, PB), PB)]

    def arrival(slot):
        return group_sems.at[GROUP_OF[slot]]

    for part in range(2):
        some = pl.ds(part * (ROWS // 2), ROWS // 2)
        for core in range(2):
            for slot in range(1, CHIPS):
                to = device(slot, core)
                send(pixels_of(to, core).at[some], rows_of(BACK[slot]).at[some], 0, to, arrival(BACK[slot]))
    to = device(0, other)
    send(pixels_of(to, other), rows_of(0), 0, to, arrival(0))
    own = pltpu.make_async_copy(pixels_of(device(0, c), c), rows_of(0), sems.at[14])
    own.start()

    begin = pltpu.make_async_copy(start.at[:, pl.ds(pl.multiple_of(c * PB, PB), PB)], initial, sems.at[15])
    begin.start()

    def share_gram(turn, partial):
        gram_out[...] = pack_gram(partial)
        send(gram_out, gram_core.at[turn], 4, device(0, other), core_sems.at[turn])

    def share_chip_gram(turn):
        wait_on(gram_core.at[turn], core_sems.at[turn])
        gram_chip[...] = gram_out[...] + gram_core[turn]
        wait(gram_out, 4)
        for slot in FAR_FIRST:
            send(gram_chip, gram_in.at[turn, BACK[slot] - 1], 6, device(slot, c), gram_sems.at[turn])

    def sum_gram(turn):
        wait_on(gram_in.at[turn], gram_sems.at[turn])
        total = gram_chip[...]
        for i in range(CHIPS - 1):
            total = total + gram_in[turn, i]
        wait(gram_in.at[turn], 6)
        return unpack_gram(total)

    def gram_of(now):
        return lax.dot_general(now, now, NT, preferred_element_type=F32)

    def send_part(turn, slot, core):
        place = BACK[slot] * 2 - 1 + c if slot else 0
        send(part1.at[slot, core], got1.at[turn, place], 2, device(slot, core), got_sems.at[turn])

    def add_up_stamps(now, turn, group, least):
        first, last = group
        partial = jnp.dot(
            now, blockt[:, first * LANES : last * LANES], preferred_element_type=F32
        ).astype(BF)
        for slot in range(first, last):
            for core in range(2):
                piece = partial[HK * core : HK * core + HK, LANES * (slot - first) : LANES * (slot - first + 1)]
                part1[slot, core, 0] = piece
                part1[slot ^ 1, core, 1] = piece
        for slot in FAR_FIRST:
            if first <= slot < last and HOPS[slot] >= least:
                for core in range(2):
                    send_part(turn, slot, core)

    def add_up_nearest(turn):
        for slot in FAR_FIRST:
            if HOPS[slot] == 1:
                for core in range(2):
                    send_part(turn, slot, core)
        send_part(turn, 0, other)

    def gather_stamps(turn):
        wait_on(got1.at[turn], got_sems.at[turn])
        total = part1[0, c].astype(F32)
        for i in range(2 * CHIPS - 1):
            total = total + got1[turn, i].astype(F32)
        proj[0, c] = total[0].astype(BF)
        proj[1, c] = total[1].astype(BF)
        both = proj.at[pl.ds(0, 2), c]
        for slot in FAR_FIRST:
            for core in range(2):
                if HOPS[slot] == 2:
                    send(proj.at[0, c], proj.at[BACK[slot], c], 8, device(slot, core), arrival(BACK[slot]))
                elif HOPS[slot] == 1:
                    send(both, proj.at[pl.ds(BACK[slot], 2), c], 8, device(slot, core), arrival(BACK[slot]))
        send(both, both, 8, device(0, other), arrival(0))
        wait(got1.at[turn], 2)

    def add_up_pixels(turn, then=None):
        back = jnp.zeros((K, PB), F32)
        for first, last in GROUPS:
            tiles = 2 * (last - first) - (2 if first == 0 else 0)
            wait_on(got1.at[0, pl.ds(0, tiles // 2)], arrival(first))
            if first == 0 and then is not None:
                then(turn)
            raw = jnp.concatenate(
                [jnp.concatenate([proj[i, 0], proj[i, 1]], axis=0) for i in range(first, last)], axis=1
            )
            back = back + jnp.dot(
                raw, block[first * LANES : last * LANES, :], preferred_element_type=F32
            )
        sums[turn, z] = back.astype(BF)
        for dz in Z_STEPS:
            send(sums.at[turn, z], sums.at[turn, z], 10, at_z(dz), z_sems.at[turn])
        wait(proj.at[pl.ds(0, CHIPS - 1)], 8)

    def sum_pixels(turn):
        wait_on(sums.at[turn, pl.ds(0, GZ - 1)], z_sems.at[turn])
        total = sums[turn, 0].astype(F32)
        for i in range(1, GZ):
            total = total + sums[turn, i].astype(F32)
        return total

    begin.wait()
    own.wait()
    now = initial[...].astype(BF)
    for group in range(len(GROUPS)):
        first, last = GROUPS[group]
        remote = (last - first) * 2 * ROWS - (ROWS if first == 0 else 0)
        wait_on(block.at[pl.ds(0, remote)], arrival(first))
        blockt[:, first * LANES : last * LANES] = block[first * LANES : last * LANES, :].T
        add_up_stamps(now, 0, GROUPS[group], 1)
        if first == 0:
            send_part(0, 0, other)
    wait(block.at[pl.ds(0, SB - ROWS)], 0)
    gather_stamps(0)
    add_up_pixels(0)

    def sweep(step, now):
        turn = lax.rem(step, 2)
        for group in PUSH:
            add_up_stamps(now, turn, group, 2)
        add_up_nearest(turn)
        wait(sums.at[0, pl.ds(0, GZ - 1)], 10)
        share_gram(turn, gram_of(now))
        gather_stamps(turn)
        add_up_pixels(turn, share_chip_gram)
        factor = inverse_cholesky(sum_gram(turn))
        return apply_factor(factor, sum_pixels(turn)).astype(BF)

    now = lax.fori_loop(1, ITERS, sweep, sum_pixels(0).astype(BF))

    wait(sums.at[0, pl.ds(0, GZ - 1)], 10)
    panel[...] = now
    send(panel, pair, 12, device(0, other))
    gram_all[0, c] = pack_gram(gram_of(now))
    for slot in FAR_FIRST:
        for core in range(2):
            send(gram_all.at[0, c], gram_all.at[BACK[slot], c], 6, device(slot, core))
    send(gram_all.at[0, c], gram_all.at[0, c], 6, device(0, other))
    wait(pair, 13)
    wait(pair, 12)
    every = got1.at[0, :, 0]
    wait(every, 7)
    wait(every, 6)
    total = gram_all[0, 0] + gram_all[0, 1]
    for slot in range(1, CHIPS):
        total = total + (gram_all[slot, 0] + gram_all[slot, 1])
    factor = inverse_cholesky(unpack_gram(total)) * SCALE
    out[:, pl.ds(pl.multiple_of(c * PB, PB), PB)] = apply_factor(factor, now.astype(F32))
    out[:, pl.ds(pl.multiple_of(other * PB, PB), PB)] = apply_factor(factor, pair[...].astype(F32))


def local(stamps, start_panel):
    vmem = pl.BlockSpec(memory_space=pltpu.VMEM)
    result = pl.pallas_call(
        kernel,
        out_shape=jax.ShapeDtypeStruct((K, PC), F32),
        in_specs=[pl.BlockSpec(memory_space=pl.ANY)] * 2,
        out_specs=vmem,
        scratch_shapes=[
            pltpu.VMEM((SB, PB), BF),
            pltpu.VMEM((PB, SB), BF),
            pltpu.VMEM((K, PB), F32),
            pltpu.VMEM((K, PB), BF),
            pltpu.VMEM((CHIPS, 2, 2, HK, LANES), BF),
            pltpu.VMEM((2, 2 * CHIPS - 1, 2, HK, LANES), BF),
            pltpu.VMEM((CHIPS, 2, HK, LANES), BF),
            pltpu.VMEM((8, LANES), F32),
            pltpu.VMEM((2, 8, LANES), F32),
            pltpu.VMEM((8, LANES), F32),
            pltpu.VMEM((2, CHIPS - 1, 8, LANES), F32),
            pltpu.VMEM((CHIPS, 2, 8, LANES), F32),
            pltpu.VMEM((2, GZ, K, PB), BF),
            pltpu.VMEM((K, PB), BF),
            pltpu.SemaphoreType.DMA((16,)),
            pltpu.SemaphoreType.DMA((len(GROUPS),)),
            pltpu.SemaphoreType.DMA((2,)),
            pltpu.SemaphoreType.DMA((2,)),
            pltpu.SemaphoreType.DMA((2,)),
            pltpu.SemaphoreType.DMA((2,)),
        ],
        compiler_params=pltpu.CompilerParams(
            collective_id=0, has_side_effects=True, vmem_limit_bytes=63 << 20
        ),
    )(stamps, start_panel.T)
    return result.T


def solution(mesh):
    return jax.shard_map(
        local,
        mesh=mesh,
        in_specs=(P(("samp", "pix"), None), P("pix", None)),
        out_specs=P("pix", None),
        check_vma=False,
    )
```
